512 devices in a mesh: tm: 4 (over x), tile: 128 (over z, y, core).
Axes of the slice: x: 4, y: 8, z: 8, core: 2. Of those that a mesh axis runs over, the one named last changes fastest.
Arguments:
- frames: bfloat16 [4, 128, 8, 16, 384], P('tm', 'tile'), may hold values from -6 to 6
- norm_gain: float32 [384], replicated, may hold values from 0.1 to 1.9
- conv_weight: bfloat16 [3, 3, 3, 384, 384], replicated, may hold values from -0.0625 to 0.0625
- conv_bias: float32 [384], replicated, may hold values from -3 to 3
Outputs:
- decoded: bfloat16 [4, 128, 8, 16, 384], P('tm', 'tile')
The draws below stay inside these ranges and needn't reach their ends.
All inputs are finite; a program needn't handle non-finite values.
Results may differ from the reference program's by a relative error of at most 0.0055.
Values may be sent and summed in bfloat16 or wider, within the bound.
A program may use at most 64 MiB of HBM per device.

```python
import jax
import jax.numpy as jnp
from jax import lax

C = 384
TH = 8
TW = 16
GRID_W = 8
FRAMES = 4
TILES = 128


def level_of(own_key, shape, split, smallest, high):
    def one(axis_at, blocks):
        draws = jax.random.uniform(jax.random.fold_in(jax.random.fold_in(own_key, 6), axis_at), (blocks,), jnp.float32, smallest / len(split), high / len(split))
        return jnp.repeat(jnp.exp(draws), shape[axis_at] // blocks).reshape((-1,) + (1,) * (len(shape) - axis_at - 1))

    loudness = one(*split[0])
    for cut in split[1:]:
        loudness = loudness * one(*cut)
    return loudness


def centred(rng, dims, spread, bound, split=(), dtype=jnp.bfloat16):
    entries = spread * jax.random.normal(rng, dims, jnp.float32)
    if split:
        entries = entries * level_of(rng, dims, split, -0.22, 0.18)
    return jnp.clip(entries, -bound, bound).astype(dtype)


def setup_inputs(seed: int = 0) -> dict:
    key_of = jax.random.split(jax.random.key(seed), 5)
    return {
        "frames": centred(key_of[0], (FRAMES, TILES, TH, TW, C), 1.0, 6.0, ((0, 4), (1, 128))),
        "norm_gain": jnp.clip(1.0 + 0.18 * jax.random.normal(key_of[1], (C,), jnp.float32), 0.1, 1.9),
        "conv_weight": centred(key_of[2], (3, 3, 3, C, C), (27 * C) ** -0.5, 0.0625),
        "conv_bias": centred(key_of[3], (C,), 0.5, 3.0, (), jnp.float32),
    }


def activate(tile_values, norm_gain):
    values = tile_values.astype(jnp.float32)
    scale = lax.rsqrt(lax.optimization_barrier(jnp.mean(values * values, axis=-1, keepdims=True)) + 1e-06)
    return jax.nn.silu(values * scale * norm_gain).astype(jnp.bfloat16)

def assemble(tiled, grid_h, grid_w):
    shaped = tiled.reshape(FRAMES, grid_h, grid_w, TH, TW, C)
    return shaped.transpose(0, 1, 3, 2, 4, 5).reshape(FRAMES, grid_h * TH, grid_w * TW, C)

def reference(frames, norm_gain, conv_weight, conv_bias):
    activation = activate(frames, norm_gain)
    grid_h = TILES // GRID_W
    whole = assemble(activation, grid_h, GRID_W).astype(jnp.float32)
    padded = jnp.pad(whole, ((2, 0), (1, 1), (1, 1), (0, 0)))
    summed = lax.conv_general_dilated(padded[None], conv_weight.astype(jnp.float32), (1, 1, 1), 'VALID', dimension_numbers=('NDHWC', 'DHWIO', 'NDHWC'), precision=lax.Precision.HIGHEST)[0]
    summed = summed + conv_bias
    shaped = summed.reshape(FRAMES, grid_h, TH, GRID_W, TW, C).transpose(0, 1, 3, 2, 4, 5)
    return shaped.reshape(FRAMES, TILES, TH, TW, C).astype(jnp.bfloat16)
```

```python
import functools

import jax
import jax.numpy as jnp
from jax import lax
from jax.experimental import pallas as pl
from jax.experimental.pallas import tpu as pltpu
from jax.sharding import PartitionSpec as P

GRID_W = 8
LANES = 128
MESH = pl.DeviceIdType.MESH
F32 = jnp.float32
BF16 = jnp.bfloat16


def block_kernel(
    tall,
    broad,
    chans,
    frame_count,
    tile_count,
    frames_hbm,
    gain_hbm,
    weight_hbm,
    bias_hbm,
    out_ref,
    raw,
    gain,
    bias,
    weight,
    tile,
    act32,
    col_out,
    col_in,
    row_in,
    corner_out,
    corner_in,
    window,
    edge_window,
    acc,
    load_sem,
    weight_sem,
    edge_send,
    edge_recv,
    mid_send,
    mid_recv,
    col_send,
    col_recv,
    row_send,
    row_recv,
    corner_send,
    corner_recv,
):
    t = lax.axis_index("tm")
    i = lax.axis_index("tile")
    row = lax.div(i, GRID_W)
    col = lax.rem(i, GRID_W)
    grid_h = tile_count // GRID_W
    pixels = tall * broad
    last = pixels - broad

    def inside(dt, dr, dc):
        ok = None
        tests = []
        if dt > 0:
            tests.append(t + dt < frame_count)
        if dt < 0:
            tests.append(t + dt >= 0)
        if dr > 0:
            tests.append(row + dr < grid_h)
        if dr < 0:
            tests.append(row + dr >= 0)
        if dc > 0:
            tests.append(col + dc < GRID_W)
        if dc < 0:
            tests.append(col + dc >= 0)
        for test in tests:
            ok = test if ok is None else jnp.logical_and(ok, test)
        return ok

    def device(dt, dr, dc):
        return {"tm": t + dt, "tile": i + dr * GRID_W + dc}

    partners = [(dt, 0, 0) for dt in (-2, -1, 1, 2)]
    partners += [(dt, 0, dc) for dt in (-2, -1, 0, 1, 2) for dc in (-1, 1)]
    partners += [(0, dr, dc) for dr in (-1, 1) for dc in (-1, 0, 1)]

    barrier = pltpu.get_barrier_semaphore()
    count = jnp.int32(0)
    for offset in partners:
        ok = inside(*offset)
        count = count + ok.astype(jnp.int32)

        @pl.when(ok)
        def _(offset=offset):
            pl.semaphore_signal(barrier, 1, device_id=device(*offset), device_id_type=MESH)

    loads = [
        pltpu.make_async_copy(frames_hbm, raw, load_sem.at[0]),
        pltpu.make_async_copy(gain_hbm, gain, load_sem.at[1]),
        pltpu.make_async_copy(bias_hbm, bias, load_sem.at[2]),
    ]
    for load in loads:
        load.start()
    weight_loads = [
        pltpu.make_async_copy(
            weight_hbm.at[pl.ds(6 - 3 * s, 3)], weight.at[pl.ds(6 - 3 * s, 3)], weight_sem.at[s]
        )
        for s in range(3)
    ]
    for load in weight_loads:
        load.start()
    for load in loads:
        load.wait()

    def activate(start, size):
        values = raw[start : start + size, :].astype(F32)
        scale = lax.rsqrt(jnp.mean(values * values, axis=-1, keepdims=True) + 1e-06)
        result = jax.nn.silu(values * scale * gain[...].reshape(1, chans)).astype(BF16)
        tile[0, start : start + size, :] = result
        for j in range(chans // LANES):
            act32[j, start : start + size, :] = result[:, j * LANES : (j + 1) * LANES].astype(F32)

    activate(0, pixels)
    for side in (0, 1):
        for j in range(chans // LANES):
            column = act32[j, pl.ds(side * (broad - 1), tall, stride=broad), :]
            col_out[side, :, j * LANES : (j + 1) * LANES] = column.astype(BF16)

    pl.semaphore_wait(barrier, count)

    def remote(src, dst, send, recv, offset):
        return pltpu.make_async_remote_copy(
            src_ref=src,
            dst_ref=dst,
            send_sem=send,
            recv_sem=recv,
            device_id=device(*offset),
            device_id_type=MESH,
        )

    edges = (pl.ds(0, broad), pl.ds(last, broad))
    middle = pl.ds(broad, pixels - 2 * broad)

    def edge_copy(s, k):
        return remote(
            tile.at[0, edges[k]], tile.at[s, edges[k]], edge_send.at[s, k], edge_recv.at[s, k], (s, 0, 0)
        )

    def mid_copy(s):
        return remote(tile.at[0, middle], tile.at[s, middle], mid_send.at[s], mid_recv.at[s], (s, 0, 0))

    def col_copy(s, side):
        return remote(
            col_out.at[side],
            col_in.at[s, 1 - side],
            col_send.at[s, side],
            col_recv.at[s, 1 - side],
            (s, 0, 2 * side - 1),
        )

    def row_copy(s, side):
        return remote(
            tile.at[s, edges[side]],
            row_in.at[s, 1 - side],
            row_send.at[s, side],
            row_recv.at[s, 1 - side],
            (0, 2 * side - 1, 0),
        )

    def corner_copy(s, side, end):
        return remote(
            corner_out.at[s, 2 * side + end],
            corner_in.at[s, 3 - 2 * side - end],
            corner_send.at[s, 2 * side + end],
            corner_recv.at[s, 3 - 2 * side - end],
            (0, 2 * side - 1, 2 * end - 1),
        )

    def guard(ok, body):
        if ok is None:
            body()
        else:
            pl.when(ok)(body)

    def started(copy, *args):
        guard(inside(*offset_of(copy, *args)), lambda: copy(*args).start())

    def offset_of(copy, *args):
        if copy is edge_copy or copy is mid_copy:
            return (args[0], 0, 0)
        if copy is col_copy:
            return (args[0], 0, 2 * args[1] - 1)
        if copy is row_copy:
            return (0, 2 * args[1] - 1, 0)
        return (0, 2 * args[1] - 1, 2 * args[2] - 1)

    for s in (2, 1):
        for k in (0, 1):
            started(edge_copy, s, k)
    for s in (2, 1, 0):
        for side in (0, 1):
            started(col_copy, s, side)
    for s in (2, 1):
        started(mid_copy, s)

    def forward(s):
        for side in (0, 1):
            started(row_copy, s, side)
        for side in (0, 1):
            edge = tile[s, edges[side], :].astype(F32)
            corner_out[s, 2 * side] = edge[0:1, :]
            corner_out[s, 2 * side + 1] = edge[broad - 1 : broad, :]
        for side in (0, 1):
            for end in (0, 1):
                started(corner_copy, s, side, end)

    forward(0)
    for s in (1, 2):

        @pl.when(t >= s)
        def _(s=s):
            for k in (0, 1):
                edge_copy(s, k).wait_recv()
            forward(s)

    along = lax.broadcasted_iota(jnp.int32, (broad, chans), 0)

    def spread(block, left, right):
        before = jnp.where(along == 0, left, pltpu.roll(block, 1, axis=0))
        after = jnp.where(along == broad - 1, right, pltpu.roll(block, broad - 1, axis=0))
        return before.astype(BF16), block.astype(BF16), after.astype(BF16)

    def dot(a, b):
        return jnp.dot(a, b, preferred_element_type=F32)

    def add_frame(s):
        for side in (0, 1):

            @pl.when(inside(0, 0, 2 * side - 1))
            def _(side=side):
                pltpu.make_async_copy(col_in.at[s, side], col_in.at[s, side], col_recv.at[s, side]).wait()

        if s > 0:
            mid_copy(s).wait_recv()
        left = jnp.where(col > 0, col_in[s, 0].astype(F32), 0.0)
        right = jnp.where(col < GRID_W - 1, col_in[s, 1].astype(F32), 0.0)
        for y in range(tall):
            rows = slice(y * broad, (y + 1) * broad)
            parts = spread(tile[s, rows, :].astype(F32), left[y : y + 1, :], right[y : y + 1, :])
            for e in range(3):
                window[rows, e * chans : (e + 1) * chans] = parts[e]
        weight_loads[s].wait()
        at = 3 * (2 - s)
        total = dot(window[...], weight[at + 1])
        if s == 0:
            acc[...] = total + bias[...].reshape(1, chans)
        else:
            acc[...] += total
        acc[broad:, :] += dot(window[:last, :], weight[at])
        acc[:last, :] += dot(window[broad:, :], weight[at + 2])

    def add_rows(s):
        for side in (0, 1):

            @pl.when(inside(0, 2 * side - 1, 0))
            def _(side=side):
                pltpu.make_async_copy(row_in.at[s, side], row_in.at[s, side], row_recv.at[s, side]).wait()
                ends = []
                for end in (0, 1):
                    k = 2 * side + end

                    @pl.when(inside(0, 0, 2 * end - 1))
                    def _(k=k):
                        pltpu.make_async_copy(corner_in.at[s, k], corner_in.at[s, k], corner_recv.at[s, k]).wait()

                    ends.append(jnp.where(inside(0, 0, 2 * end - 1), corner_in[s, k], 0.0))
                parts = spread(row_in[s, side].astype(F32), *ends)
                for e in range(3):
                    edge_window[side, :, e * chans : (e + 1) * chans] = parts[e]
                acc[edges[side], :] += dot(edge_window[side], weight[3 * (2 - s) + 2 * side])

    add_frame(0)
    for s in (1, 2):
        pl.when(t >= s)(functools.partial(add_frame, s))

        @pl.when(t < s)
        def _(s=s):
            weight_loads[s].wait()

    add_rows(0)
    for s in (1, 2):
        pl.when(t >= s)(functools.partial(add_rows, s))

    out_ref[...] = acc[...].astype(BF16)

    def sent(copy, *args):
        guard(inside(*offset_of(copy, *args)), lambda: copy(*args).wait_send())

    for s in (2, 1):
        for k in (0, 1):
            sent(edge_copy, s, k)
        sent(mid_copy, s)
    for s in (2, 1, 0):
        for side in (0, 1):
            sent(col_copy, s, side)

    def forwarded(s):
        for side in (0, 1):
            sent(row_copy, s, side)
            for end in (0, 1):
                sent(corner_copy, s, side, end)

    forwarded(0)
    for s in (1, 2):
        pl.when(t >= s)(functools.partial(forwarded, s))


def solution(mesh):
    frame_count = mesh.shape["tm"]
    tile_count = mesh.shape["tile"]

    def body(frames, norm_gain, conv_weight, conv_bias):
        _, _, tall, broad, chans = frames.shape
        pixels = tall * broad
        out = pl.pallas_call(
            functools.partial(block_kernel, tall, broad, chans, frame_count, tile_count),
            name="causal_conv",
            out_shape=pltpu.VMEM((pixels, chans), BF16),
            in_specs=[pl.BlockSpec(memory_space=pl.ANY)] * 4,
            out_specs=pl.BlockSpec(memory_space=pltpu.VMEM),
            scratch_shapes=[
                pltpu.VMEM((pixels, chans), BF16),
                pltpu.VMEM((chans,), F32),
                pltpu.VMEM((chans,), F32),
                pltpu.VMEM((9, 3 * chans, chans), BF16),
                pltpu.VMEM((3, pixels, chans), BF16),
                pltpu.VMEM((chans // LANES, pixels, LANES), F32),
                pltpu.VMEM((2, tall, chans), BF16),
                pltpu.VMEM((3, 2, tall, chans), BF16),
                pltpu.VMEM((3, 2, broad, chans), BF16),
                pltpu.VMEM((3, 4, 1, chans), F32),
                pltpu.VMEM((3, 4, 1, chans), F32),
                pltpu.VMEM((pixels, 3 * chans), BF16),
                pltpu.VMEM((2, broad, 3 * chans), BF16),
                pltpu.VMEM((pixels, chans), F32),
                pltpu.SemaphoreType.DMA((3,)),
                pltpu.SemaphoreType.DMA((3,)),
                pltpu.SemaphoreType.DMA((3, 2)),
                pltpu.SemaphoreType.DMA((3, 2)),
                pltpu.SemaphoreType.DMA((3,)),
                pltpu.SemaphoreType.DMA((3,)),
                pltpu.SemaphoreType.DMA((3, 2)),
                pltpu.SemaphoreType.DMA((3, 2)),
                pltpu.SemaphoreType.DMA((3, 2)),
                pltpu.SemaphoreType.DMA((3, 2)),
                pltpu.SemaphoreType.DMA((3, 4)),
                pltpu.SemaphoreType.DMA((3, 4)),
            ],
            compiler_params=pltpu.CompilerParams(collective_id=0, has_side_effects=True),
        )(
            frames.reshape(pixels, chans),
            norm_gain,
            conv_weight.reshape(9, 3 * chans, chans),
            conv_bias,
        )
        return out.reshape(1, 1, tall, broad, chans)

    return jax.shard_map(
        body,
        mesh=mesh,
        in_specs=(P("tm", "tile", None, None, None), P(), P(), P()),
        out_specs=P("tm", "tile", None, None, None),
        check_vma=False,
    )
```

```python
import functools

import jax
import jax.numpy as jnp
from jax import lax
from jax.experimental import pallas as pl
from jax.experimental.pallas import tpu as pltpu
from jax.sharding import PartitionSpec as P

GRID_W = 8
LANES = 128
RING_Y = 8
MESH = pl.DeviceIdType.MESH
F32 = jnp.float32
BF16 = jnp.bfloat16


def block_kernel(
    tall,
    broad,
    chans,
    frame_count,
    tile_count,
    frames_hbm,
    gain_hbm,
    weight_hbm,
    bias_hbm,
    out_ref,
    raw,
    gain,
    bias,
    weight,
    tile,
    act32,
    col_out,
    col_in,
    row_in,
    corner_out,
    corner_in,
    window,
    side_window,
    acc,
    load_sem,
    weight_sem,
    far_sem,
    edge_send,
    edge_recv,
    mid_send,
    mid_recv,
    col_send,
    col_recv,
    row_send,
    row_recv,
    corner_send,
    corner_recv,
):
    t = lax.axis_index("tm")
    i = lax.axis_index("tile")
    row = lax.div(i, GRID_W)
    col = lax.rem(i, GRID_W)
    grid_h = tile_count // GRID_W
    pixels = tall * broad
    last = pixels - broad

    loads = [
        pltpu.make_async_copy(frames_hbm, raw, load_sem.at[0]),
        pltpu.make_async_copy(gain_hbm, gain, load_sem.at[1]),
        pltpu.make_async_copy(bias_hbm, bias, load_sem.at[2]),
    ]
    for load in loads:
        load.start()

    def inside(dt, dr, dc):
        tests = []
        if dt > 0:
            tests.append(t + dt < frame_count)
        if dt < 0:
            tests.append(t + dt >= 0)
        if dr > 0:
            tests.append(row + dr < grid_h)
        if dr < 0:
            tests.append(row + dr >= 0)
        if dc > 0:
            tests.append(col + dc < GRID_W)
        if dc < 0:
            tests.append(col + dc >= 0)
        return functools.reduce(jnp.logical_and, tests)

    def signal(sem, dt, index):
        pl.semaphore_signal(sem, 1, device_id={"tm": t + dt, "tile": index}, device_id_type=MESH)

    def along_y(index, by):
        return lax.div(index, 2 * RING_Y) * 2 * RING_Y + lax.rem(index + 2 * by + 2 * RING_Y, 2 * RING_Y)

    barrier = pltpu.get_barrier_semaphore()
    count = jnp.int32(1)
    for dr in (-1, 1):
        pl.when(inside(0, dr, 0))(functools.partial(signal, barrier, 0, along_y(i + dr * GRID_W, 2)))
    signal(barrier, 0, along_y(i, 2))
    told = along_y(i, -2)
    told_row = lax.div(told, GRID_W)
    count = count + (told_row > 0).astype(jnp.int32) + (told_row < grid_h - 1).astype(jnp.int32)
    partners = [(dt, dc) for dt in (-2, 2, -1, 1, 0) for dc in (-1, 1)]
    partners += [(dt, 0) for dt in (-2, 2, -1, 1)]
    for dt, dc in partners:
        ok = inside(dt, 0, dc)
        count = count + ok.astype(jnp.int32)
        pl.when(ok)(functools.partial(signal, barrier, dt, i + dc))

    weight_loads = [
        pltpu.make_async_copy(
            weight_hbm.at[pl.ds(6 - 3 * s, 3)], weight.at[pl.ds(6 - 3 * s, 3)], weight_sem.at[s]
        )
        for s in range(3)
    ]
    for load in weight_loads:
        load.start()

    loads[0].wait()
    loads[1].wait()

    values = raw[...].astype(F32)
    scale = lax.rsqrt(jnp.mean(values * values, axis=-1, keepdims=True) + 1e-06)
    result = jax.nn.silu(values * scale * gain[...].reshape(1, chans)).astype(BF16)
    tile[0] = result
    for j in range(chans // LANES):
        lanes = slice(j * LANES, (j + 1) * LANES)
        act32[j] = result[:, lanes].astype(F32)
        for side in (0, 1):
            column = act32[j, pl.ds(side * (broad - 1), tall, stride=broad), :]
            col_out[side, :, lanes] = column.astype(BF16)

    pl.semaphore_wait(barrier, count)
    signal(far_sem, 0, told)

    def remote(src, dst, send, recv, offset):
        dt, dr, dc = offset
        return pltpu.make_async_remote_copy(
            src_ref=src,
            dst_ref=dst,
            send_sem=send,
            recv_sem=recv,
            device_id={"tm": t + dt, "tile": i + dr * GRID_W + dc},
            device_id_type=MESH,
        )

    edges = (pl.ds(0, broad), pl.ds(last, broad))
    middle = pl.ds(broad, pixels - 2 * broad)

    def edge_copy(s, k):
        offset = (s, 0, 0)
        return remote(tile.at[0, edges[k]], tile.at[s, edges[k]], edge_send.at[s, k], edge_recv.at[s, k], offset), offset

    def mid_copy(s):
        offset = (s, 0, 0)
        return remote(tile.at[0, middle], tile.at[s, middle], mid_send.at[s], mid_recv.at[s], offset), offset

    def col_copy(s, side):
        offset = (s, 0, 2 * side - 1)
        return remote(col_out.at[side], col_in.at[s, 1 - side], col_send.at[s, side], col_recv.at[s, 1 - side], offset), offset

    def row_copy(s, side):
        offset = (0, 2 * side - 1, 0)
        return remote(tile.at[s, edges[side]], row_in.at[s, 1 - side], row_send.at[s, side], row_recv.at[s, 1 - side], offset), offset

    def corner_copy(s, side):
        offset = (0, 2 * side - 1, 0)
        return remote(corner_out.at[s, side], corner_in.at[s, 1 - side], corner_send.at[s, side], corner_recv.at[s, 1 - side], offset), offset

    def start(copy, *args):
        made, offset = copy(*args)
        pl.when(inside(*offset))(made.start)

    def sent(copy, *args):
        made, offset = copy(*args)
        pl.when(inside(*offset))(made.wait_send)

    def arrived(ref, sem):
        pltpu.make_async_copy(ref, ref, sem).wait()

    for s in (2, 1):
        for k in (0, 1):
            start(edge_copy, s, k)
        for side in (0, 1):
            start(col_copy, s, side)
    for side in (0, 1):
        start(col_copy, 0, side)
    for s in (2, 1):
        start(mid_copy, s)

    pl.semaphore_wait(far_sem, 1)

    def send_rows(s):
        for side in (0, 1):
            start(row_copy, s, side)

    def send_corners(s):
        for end in (0, 1):
            pl.when(inside(0, 0, 2 * end - 1))(
                functools.partial(arrived, col_in.at[s, end], col_recv.at[s, end])
            )
        for end in (0, 1):
            column = jnp.where(inside(0, 0, 2 * end - 1), col_in[s, end].astype(F32), 0.0)
            corner_out[s, 0, end] = column[0:1, :]
            corner_out[s, 1, end] = column[tall - 1 : tall, :]
        for side in (0, 1):
            start(corner_copy, s, side)

    send_rows(0)
    send_corners(0)
    for s in (1, 2):

        @pl.when(t >= s)
        def _(s=s):
            for k in (0, 1):
                edge_copy(s, k)[0].wait_recv()
            send_rows(s)
            send_corners(s)

    along = lax.broadcasted_iota(jnp.int32, (broad, chans), 0)

    def spread(block, left, right):
        before = jnp.where(along == 0, left, pltpu.roll(block, 1, axis=0))
        after = jnp.where(along == broad - 1, right, pltpu.roll(block, broad - 1, axis=0))
        return before.astype(BF16), block.astype(BF16), after.astype(BF16)

    def dot(a, b):
        return jnp.dot(a, b, preferred_element_type=F32)

    def add_tile(s):
        if s > 0:
            mid_copy(s)[0].wait_recv()
        left, right = (
            jnp.where(inside(0, 0, 2 * end - 1), col_in[s, end].astype(F32), 0.0) for end in (0, 1)
        )
        for y in range(tall):
            rows = slice(y * broad, (y + 1) * broad)
            parts = spread(tile[s, rows, :].astype(F32), left[y : y + 1, :], right[y : y + 1, :])
            for e in range(3):
                window[rows, e * chans : (e + 1) * chans] = parts[e]
        weight_loads[s].wait()
        at = 6 - 3 * s
        total = dot(window[...], weight[at + 1])
        if s == 0:
            acc[...] = total + bias[...].reshape(1, chans)
        else:
            acc[...] += total
        acc[broad:, :] += dot(window[:last, :], weight[at])
        acc[:last, :] += dot(window[broad:, :], weight[at + 2])

    def add_rows(s):
        for side in (0, 1):

            @pl.when(inside(0, 2 * side - 1, 0))
            def _(side=side):
                arrived(row_in.at[s, side], row_recv.at[s, side])
                arrived(corner_in.at[s, side], corner_recv.at[s, side])

        for side in (0, 1):
            there = inside(0, 2 * side - 1, 0)
            halo = jnp.where(there, row_in[s, side].astype(F32), 0.0)
            ends = [
                jnp.where(jnp.logical_and(there, inside(0, 0, 2 * end - 1)), corner_in[s, side, end], 0.0)
                for end in (0, 1)
            ]
            parts = spread(halo, *ends)
            for e in range(3):
                side_window[side, :, e * chans : (e + 1) * chans] = parts[e]
        for side in (0, 1):
            acc[edges[side], :] += dot(side_window[side], weight[6 - 3 * s + 2 * side])

    loads[2].wait()
    add_tile(0)
    for s in (1, 2):
        pl.when(t >= s)(functools.partial(add_tile, s))
        pl.when(t < s)(weight_loads[s].wait)

    for s in (2, 1):
        for k in (0, 1):
            sent(edge_copy, s, k)
        sent(mid_copy, s)
    for s in (2, 1, 0):
        for side in (0, 1):
            sent(col_copy, s, side)

    def forwarded(s):
        for side in (0, 1):
            sent(row_copy, s, side)
            sent(corner_copy, s, side)

    forwarded(0)
    for s in (1, 2):
        pl.when(t >= s)(functools.partial(forwarded, s))

    inner = slice(broad, last)
    out_ref[inner, :] = acc[inner, :].astype(BF16)
    add_rows(0)
    for s in (1, 2):
        pl.when(t >= s)(functools.partial(add_rows, s))
    for side in (0, 1):
        out_ref[edges[side], :] = acc[edges[side], :].astype(BF16)


def solution(mesh):
    frame_count = mesh.shape["tm"]
    tile_count = mesh.shape["tile"]

    def body(frames, norm_gain, conv_weight, conv_bias):
        _, _, tall, broad, chans = frames.shape
        pixels = tall * broad
        out = pl.pallas_call(
            functools.partial(block_kernel, tall, broad, chans, frame_count, tile_count),
            name="causal_conv",
            out_shape=pltpu.VMEM((pixels, chans), BF16),
            in_specs=[pl.BlockSpec(memory_space=pl.ANY)] * 4,
            out_specs=pl.BlockSpec(memory_space=pltpu.VMEM),
            scratch_shapes=[
                pltpu.VMEM((pixels, chans), BF16),
                pltpu.VMEM((chans,), F32),
                pltpu.VMEM((chans,), F32),
                pltpu.VMEM((9, 3 * chans, chans), BF16),
                pltpu.VMEM((3, pixels, chans), BF16),
                pltpu.VMEM((chans // LANES, pixels, LANES), F32),
                pltpu.VMEM((2, tall, chans), BF16),
                pltpu.VMEM((3, 2, tall, chans), BF16),
                pltpu.VMEM((3, 2, broad, chans), BF16),
                pltpu.VMEM((3, 2, 2, 1, chans), F32),
                pltpu.VMEM((3, 2, 2, 1, chans), F32),
                pltpu.VMEM((pixels, 3 * chans), BF16),
                pltpu.VMEM((2, broad, 3 * chans), BF16),
                pltpu.VMEM((pixels, chans), F32),
                pltpu.SemaphoreType.DMA((3,)),
                pltpu.SemaphoreType.DMA((3,)),
                pltpu.SemaphoreType.REGULAR,
                pltpu.SemaphoreType.DMA((3, 2)),
                pltpu.SemaphoreType.DMA((3, 2)),
                pltpu.SemaphoreType.DMA((3,)),
                pltpu.SemaphoreType.DMA((3,)),
                pltpu.SemaphoreType.DMA((3, 2)),
                pltpu.SemaphoreType.DMA((3, 2)),
                pltpu.SemaphoreType.DMA((3, 2)),
                pltpu.SemaphoreType.DMA((3, 2)),
                pltpu.SemaphoreType.DMA((3, 2)),
                pltpu.SemaphoreType.DMA((3, 2)),
            ],
            compiler_params=pltpu.CompilerParams(collective_id=0, has_side_effects=True),
        )(
            frames.reshape(pixels, chans),
            norm_gain,
            conv_weight.reshape(9, 3 * chans, chans),
            conv_bias,
        )
        return out.reshape(1, 1, tall, broad, chans)

    return jax.shard_map(
        body,
        mesh=mesh,
        in_specs=(P("tm", "tile", None, None, None), P(), P(), P()),
        out_specs=P("tm", "tile", None, None, None),
        check_vma=False,
    )
```

```python
import functools

import jax
import jax.numpy as jnp
from jax import lax
from jax.experimental import pallas as pl
from jax.experimental.pallas import tpu as pltpu
from jax.sharding import PartitionSpec as P

GRID_W = 8
LANES = 128
MESH = pl.DeviceIdType.MESH
F32 = jnp.float32
BF16 = jnp.bfloat16


def block_kernel(
    tall,
    broad,
    chans,
    frame_count,
    tile_count,
    frames_hbm,
    gain_hbm,
    weight_hbm,
    bias_hbm,
    out_ref,
    raw,
    gain,
    bias,
    weight,
    tile,
    act32,
    col_out,
    col_in,
    corner_out,
    corner_in,
    part_out,
    part_in,
    window,
    acc,
    part,
    load_sem,
    weight_sem,
    far_sem,
    tile_send,
    edge_recv,
    mid_recv,
    side_send,
    corner_recv,
    col_recv,
    part_send,
    part_recv,
):
    t = lax.axis_index("tm")
    i = lax.axis_index("tile")
    row = lax.div(i, GRID_W)
    col = lax.rem(i, GRID_W)
    grid_h = tile_count // GRID_W
    pixels = tall * broad
    last = pixels - broad
    half = lax.rem(row, 2)

    loads = [
        pltpu.make_async_copy(frames_hbm, raw, load_sem.at[0]),
        pltpu.make_async_copy(gain_hbm, gain, load_sem.at[1]),
        pltpu.make_async_copy(bias_hbm, bias, load_sem.at[1]),
    ]
    for load in loads:
        load.start()

    def inside(dt, dr, dc):
        tests = []
        if dt > 0:
            tests.append(t + dt < frame_count)
        if dt < 0:
            tests.append(t + dt >= 0)
        if dr > 0:
            tests.append(row + dr < grid_h)
        if dr < 0:
            tests.append(row + dr >= 0)
        if dc > 0:
            tests.append(col + dc < GRID_W)
        if dc < 0:
            tests.append(col + dc >= 0)
        return functools.reduce(jnp.logical_and, tests)

    def signal(sem, dt, index):
        pl.semaphore_signal(sem, 1, device_id={"tm": t + dt, "tile": index}, device_id_type=MESH)

    barrier = pltpu.get_barrier_semaphore()
    partners = [(dt, dc) for dt in (-2, 2) for dc in (-1, 1)]
    partners += [(dt, 0) for dt in (-2, 2)]
    partners += [(dt, dc) for dt in (-1, 1, 0) for dc in (-1, 1)]
    partners += [(dt, 0) for dt in (-1, 1)]
    beyond = jnp.logical_and(half == 1, row < grid_h - 1)
    signal(barrier, 0, i + GRID_W // 2 * (1 - 2 * half))
    signal(barrier, 0, jnp.where(beyond, i + 3 * GRID_W // 2, i))
    for dt, dc in partners:
        ok = inside(dt, 0, dc)
        signal(barrier, jnp.where(ok, dt, 0), jnp.where(ok, i + dc, i))
    place = lax.rem(i, 2 * GRID_W)
    half_way = jnp.logical_and(place >= GRID_W // 2, place < 3 * GRID_W // 2)
    above = i >= 2 * GRID_W
    met = 2 + above.astype(jnp.int32)
    count = len(partners) + jnp.logical_not(beyond).astype(jnp.int32) + jnp.where(half_way, met, 0)

    weight_loads = [
        pltpu.make_async_copy(
            weight_hbm.at[pl.ds(6 - 3 * s, 3)], weight.at[pl.ds(6 - 3 * s, 3)], weight_sem.at[0]
        )
        for s in range(3)
    ]
    for load in weight_loads:
        load.start()

    def arrived(ref, sem):
        pltpu.make_async_copy(ref, ref, sem).wait()

    loads[0].wait()
    arrived(corner_in.at[pl.ds(0, 2)], load_sem.at[1])

    values = raw[...].astype(F32)
    scale = lax.rsqrt(jnp.mean(values * values, axis=-1, keepdims=True) + 1e-06)
    result = jax.nn.silu(values * scale * gain[...].reshape(1, chans)).astype(BF16)
    tile[0, :broad, :] = result[:broad]
    tile[0, broad : 2 * broad, :] = result[last:]
    tile[0, 2 * broad :, :] = result[broad:last]
    for j in range(chans // LANES):
        lanes = slice(j * LANES, (j + 1) * LANES)
        act32[j] = result[:, lanes].astype(F32)
        for side in (0, 1):
            column = act32[j, pl.ds(side * (broad - 1), tall, stride=broad), :]
            col_out[side, :, lanes] = column.astype(BF16)
            corner_out[2 * side, :, lanes] = column[0:1, :]
            corner_out[2 * side + 1, :, lanes] = column[tall - 1 : tall, :]

    pl.semaphore_wait(barrier, count)

    @pl.when(half_way)
    def _():
        for by in (-GRID_W // 2, GRID_W // 2):
            signal(far_sem, 0, i + by)
        pl.when(above)(functools.partial(signal, far_sem, 0, i - 3 * GRID_W // 2))


    def remote(src, dst, send, recv, offset):
        dt, dr, dc = offset
        return pltpu.make_async_remote_copy(
            src_ref=src,
            dst_ref=dst,
            send_sem=send,
            recv_sem=recv,
            device_id={"tm": t + dt, "tile": i + dr * GRID_W + dc},
            device_id_type=MESH,
        )

    edges = pl.ds(0, 2 * broad)
    middle = pl.ds(2 * broad, pixels - 2 * broad)

    def edge_copy(s):
        offset = (s, 0, 0)
        return remote(tile.at[0, edges], tile.at[s, edges], tile_send.at[s - 1], edge_recv.at[s - 1], offset), offset

    def mid_copy(s):
        offset = (s, 0, 0)
        return remote(tile.at[0, middle], tile.at[s, middle], tile_send.at[s - 1], mid_recv.at[s - 1], offset), offset

    def col_copy(s, side):
        offset = (s, 0, 2 * side - 1)
        return remote(col_out.at[side], col_in.at[s, 1 - side], side_send.at[s, side], col_recv.at[s, 1 - side], offset), offset

    def corners(s, end):
        return pl.ds(4 * (s - 1) + 2 * end, 2)

    def corner_copy(s, side):
        offset = (s, 0, 2 * side - 1)
        return remote(
            corner_out.at[pl.ds(2 * side, 2)],
            corner_in.at[corners(s, 1 - side)],
            side_send.at[s, side],
            corner_recv.at[s - 1, 1 - side],
            offset,
        ), offset

    def part_copy(side):
        offset = (0, 2 * side - 1, 0)
        return remote(part_out.at[side], part_in.at[1 - side], part_send.at[side], part_recv.at[1 - side], offset), offset

    def start(copy, *args):
        made, offset = copy(*args)
        pl.when(inside(*offset))(made.start)

    for s in (2, 1):
        for side in (0, 1):
            start(corner_copy, s, side)
        start(edge_copy, s)
    for side in (0, 1):
        start(col_copy, 0, side)
    for s in (2, 1):
        for side in (0, 1):
            start(col_copy, s, side)
    for s in (2, 1):
        start(mid_copy, s)

    along = lax.broadcasted_iota(jnp.int32, (broad, chans), 0)

    def dot(a, b):
        return jnp.dot(a, b, preferred_element_type=F32)

    def spread(ref, to, s, y, beside):
        slot = {0: 0, tall - 1: 1}.get(y, y + 1)
        block = tile[s, slot * broad : (slot + 1) * broad, :].astype(F32)
        left, right = (jnp.where(inside(0, 0, 2 * end - 1), beside[end], 0.0) for end in (0, 1))
        before = jnp.where(along == 0, left, pltpu.roll(block, 1, axis=0))
        after = jnp.where(along == broad - 1, right, pltpu.roll(block, broad - 1, axis=0))
        taps = [value.astype(BF16) for value in (before, block, after)]
        if ref is None:
            return jnp.concatenate(taps, axis=1)
        for e in range(3):
            ref[to : to + broad, e * chans : (e + 1) * chans] = taps[e]

    def wait_columns(s):
        for end in (0, 1):
            pl.when(inside(0, 0, 2 * end - 1))(
                functools.partial(arrived, col_in.at[s, end], col_recv.at[s, end])
            )

    def add_part(s):
        sums = []
        for side, y in ((0, 0), (1, tall - 1)):
            if s == 0:
                beside = [col_in[0, end, y : y + 1, :].astype(F32) for end in (0, 1)]
            else:
                beside = [corner_in[4 * (s - 1) + 2 * end + side] for end in (0, 1)]
            sums.append(dot(spread(None, None, s, y, beside), weight[8 - 3 * s - 2 * side]))
        above, below = sums
        if s == 0:
            part[0] = above
            part[1] = below
        else:
            part[0] += above
            part[1] += below

    def add_tile(s):
        for y in range(tall):
            spread(window, y * broad, s, y, [col_in[s, end, y : y + 1, :].astype(F32) for end in (0, 1)])
        at = 6 - 3 * s
        total = dot(window[...], weight[at + 1])
        if s == 0:
            acc[...] = total + bias[...].reshape(1, chans)
        else:
            acc[...] += total
        acc[broad:, :] += dot(window[:last, :], weight[at])
        acc[:last, :] += dot(window[broad:, :], weight[at + 2])

    wait_columns(0)
    arrived(weight, weight_sem.at[0])
    add_part(0)
    for s in (1, 2):

        @pl.when(t >= s)
        def _(s=s):
            arrived(tile.at[s, edges], edge_recv.at[s - 1])
            for end in (0, 1):
                pl.when(inside(0, 0, 2 * end - 1))(
                    functools.partial(arrived, corner_in.at[corners(s, end)], corner_recv.at[s - 1, end])
                )
            add_part(s)

    part_out[...] = part[...].astype(BF16)
    pl.semaphore_wait(far_sem, 1 + beyond.astype(jnp.int32))
    for side in (0, 1):
        start(part_copy, side)

    add_tile(0)
    for s in (1, 2):

        @pl.when(t >= s)
        def _(s=s):
            wait_columns(s)
            arrived(tile.at[s, middle], mid_recv.at[s - 1])
            add_tile(s)

    inner = slice(broad, last)
    out_ref[inner, :] = acc[inner, :].astype(BF16)

    def sent(ref, sem, offset):
        pl.when(inside(*offset))(functools.partial(arrived, ref, sem))

    for s in (1, 2):
        sent(tile.at[0], tile_send.at[s - 1], (s, 0, 0))
    for side in (0, 1):
        sent(col_out.at[side], side_send.at[0, side], (0, 0, 2 * side - 1))
        for s in (1, 2):
            sent(corner_in.at[pl.ds(0, 2 + tall // 2)], side_send.at[s, side], (s, 0, 2 * side - 1))
        sent(part_out.at[side], part_send.at[side], (0, 2 * side - 1, 0))

    for side in (0, 1):
        there = inside(0, 2 * side - 1, 0)
        rows = slice(side * last, side * last + broad)
        pl.when(there)(functools.partial(arrived, part_in.at[side], part_recv.at[side]))
        halo = jnp.where(there, part_in[side].astype(F32), 0.0)
        out_ref[rows, :] = (acc[rows, :] + halo).astype(BF16)


def solution(mesh):
    frame_count = mesh.shape["tm"]
    tile_count = mesh.shape["tile"]

    def body(frames, norm_gain, conv_weight, conv_bias):
        _, _, tall, broad, chans = frames.shape
        pixels = tall * broad
        out = pl.pallas_call(
            functools.partial(block_kernel, tall, broad, chans, frame_count, tile_count),
            name="causal_conv",
            out_shape=pltpu.VMEM((pixels, chans), BF16),
            in_specs=[pl.BlockSpec(memory_space=pl.ANY)] * 4,
            out_specs=pl.BlockSpec(memory_space=pltpu.VMEM),
            scratch_shapes=[
                pltpu.VMEM((pixels, chans), BF16),
                pltpu.VMEM((chans,), F32),
                pltpu.VMEM((chans,), F32),
                pltpu.VMEM((9, 3 * chans, chans), BF16),
                pltpu.VMEM((3, pixels, chans), BF16),
                pltpu.VMEM((chans // LANES, pixels, LANES), F32),
                pltpu.VMEM((2, tall, chans), BF16),
                pltpu.VMEM((3, 2, tall, chans), BF16),
                pltpu.VMEM((4, 1, chans), F32),
                pltpu.VMEM((8, 1, chans), F32),
                pltpu.VMEM((2, broad, chans), BF16),
                pltpu.VMEM((2, broad, chans), BF16),
                pltpu.VMEM((pixels, 3 * chans), BF16),
                pltpu.VMEM((pixels, chans), F32),
                pltpu.VMEM((2, broad, chans), F32),
                pltpu.SemaphoreType.DMA((2,)),
                pltpu.SemaphoreType.DMA((1,)),
                pltpu.SemaphoreType.REGULAR,
                pltpu.SemaphoreType.DMA((2,)),
                pltpu.SemaphoreType.DMA((2,)),
                pltpu.SemaphoreType.DMA((2,)),
                pltpu.SemaphoreType.DMA((3, 2)),
                pltpu.SemaphoreType.DMA((2, 2)),
                pltpu.SemaphoreType.DMA((3, 2)),
                pltpu.SemaphoreType.DMA((2,)),
                pltpu.SemaphoreType.DMA((2,)),
            ],
            compiler_params=pltpu.CompilerParams(collective_id=0, has_side_effects=True),
        )(
            frames.reshape(pixels, chans),
            norm_gain,
            conv_weight.reshape(9, 3 * chans, chans),
            conv_bias,
        )
        return out.reshape(1, 1, tall, broad, chans)

    return jax.shard_map(
        body,
        mesh=mesh,
        in_specs=(P("tm", "tile", None, None, None), P(), P(), P()),
        out_specs=P("tm", "tile", None, None, None),
        check_vma=False,
    )
```

```python
import functools

import jax
import jax.numpy as jnp
from jax import lax
from jax.experimental import pallas as pl
from jax.experimental.pallas import tpu as pltpu
from jax.sharding import PartitionSpec as P

GRID_W = 8
LANES = 128
MESH = pl.DeviceIdType.MESH
F32 = jnp.float32
BF16 = jnp.bfloat16


def block_kernel(
    tall,
    broad,
    chans,
    frame_count,
    tile_count,
    frames_hbm,
    gain_hbm,
    weight_hbm,
    bias_hbm,
    out_ref,
    raw,
    gain,
    bias,
    weight,
    tile,
    act32,
    col_out,
    col_in,
    corner_out,
    corner_in,
    part_out,
    part_in,
    window,
    acc,
    part,
    load_sem,
    weight_sem,
    far_sem,
    tile_send,
    edge_recv,
    mid_recv,
    side_send,
    corner_recv,
    col_recv,
    part_send,
    part_recv,
):
    t = lax.axis_index("tm")
    i = lax.axis_index("tile")
    row = lax.div(i, GRID_W)
    col = lax.rem(i, GRID_W)
    grid_h = tile_count // GRID_W
    pixels = tall * broad
    last = pixels - broad
    half = lax.rem(row, 2)

    loads = [
        pltpu.make_async_copy(frames_hbm, raw, load_sem.at[0]),
        pltpu.make_async_copy(gain_hbm, gain, load_sem.at[1]),
        pltpu.make_async_copy(bias_hbm, bias, load_sem.at[1]),
    ]
    for load in loads:
        load.start()

    def inside(dt, dr, dc):
        tests = []
        if dt > 0:
            tests.append(t + dt < frame_count)
        if dt < 0:
            tests.append(t + dt >= 0)
        if dr > 0:
            tests.append(row + dr < grid_h)
        if dr < 0:
            tests.append(row + dr >= 0)
        if dc > 0:
            tests.append(col + dc < GRID_W)
        if dc < 0:
            tests.append(col + dc >= 0)
        return functools.reduce(jnp.logical_and, tests)

    def signal(sem, dt, index):
        pl.semaphore_signal(sem, 1, device_id={"tm": t + dt, "tile": index}, device_id_type=MESH)

    barrier = pltpu.get_barrier_semaphore()
    partners = [(dt, dc) for dt in (-2, 2) for dc in (-1, 1)]
    partners += [(dt, 0) for dt in (-2, 2)]
    partners += [(dt, dc) for dt in (-1, 1, 0) for dc in (-1, 1)]
    partners += [(dt, 0) for dt in (-1, 1)]
    odd = half == 1
    beyond = jnp.logical_and(odd, row < grid_h - 1)
    above = i >= 2 * GRID_W
    step = GRID_W // 2
    place = lax.rem(i, 2 * GRID_W)
    half_way = jnp.logical_and(place >= step, place < 3 * step)
    signal(barrier, 0, jnp.where(odd, i - step, i + step))
    signal(barrier, 0, jnp.where(odd, jnp.where(beyond, i + 3 * step, i), jnp.where(above, i + 2 * step, i)))
    signal(barrier, 0, jnp.where(beyond, i + 4 * step, i))
    for dt, dc in partners:
        ok = inside(dt, 0, dc)
        signal(barrier, jnp.where(ok, dt, 0), jnp.where(ok, i + dc, i))
    count = len(partners) + jnp.where(odd, 0, jnp.where(above, 1, 2)) + jnp.where(jnp.logical_and(odd, jnp.logical_not(beyond)), 2, 0)
    count += jnp.where(half_way, 2 + above.astype(jnp.int32), 0)
    count += jnp.where(jnp.logical_and(odd, above), 2, 0)

    weight_loads = [
        pltpu.make_async_copy(
            weight_hbm.at[pl.ds(6 - 3 * s, 3)], weight.at[pl.ds(6 - 3 * s, 3)], weight_sem.at[0]
        )
        for s in range(3)
    ]
    for load in weight_loads:
        load.start()

    def arrived(ref, sem):
        pltpu.make_async_copy(ref, ref, sem).wait()

    loads[0].wait()
    arrived(corner_in.at[pl.ds(0, 2)], load_sem.at[1])

    values = raw[...].astype(F32)
    scale = lax.rsqrt(jnp.mean(values * values, axis=-1, keepdims=True) + 1e-06)
    result = jax.nn.silu(values * scale * gain[...].reshape(1, chans)).astype(BF16)
    tile[0, :broad, :] = result[:broad]
    tile[0, broad : 2 * broad, :] = result[last:]
    tile[0, 2 * broad :, :] = result[broad:last]
    for j in range(chans // LANES):
        lanes = slice(j * LANES, (j + 1) * LANES)
        act32[j] = result[:, lanes].astype(F32)
        for side in (0, 1):
            column = act32[j, pl.ds(side * (broad - 1), tall, stride=broad), :]
            col_out[side, :, lanes] = column.astype(BF16)
            corner_out[2 * side, :, lanes] = column[0:1, :]
            corner_out[2 * side + 1, :, lanes] = column[tall - 1 : tall, :]

    pl.semaphore_wait(barrier, count)

    pl.when(half_way)(functools.partial(signal, far_sem, 0, i - step))
    pl.when(jnp.logical_and(half_way, jnp.logical_not(above)))(functools.partial(signal, far_sem, 0, i + step))
    pl.when(jnp.logical_and(odd, above))(functools.partial(signal, far_sem, 0, i - 4 * step))

    def remote(src, dst, send, recv, offset):
        dt, dr, dc = offset
        return pltpu.make_async_remote_copy(
            src_ref=src,
            dst_ref=dst,
            send_sem=send,
            recv_sem=recv,
            device_id={"tm": t + dt, "tile": i + dr * GRID_W + dc},
            device_id_type=MESH,
        )

    edges = pl.ds(0, 2 * broad)
    middle = pl.ds(2 * broad, pixels - 2 * broad)

    def edge_copy(s):
        offset = (s, 0, 0)
        return remote(tile.at[0, edges], tile.at[s, edges], tile_send.at[s - 1], edge_recv.at[s - 1], offset), offset

    def mid_copy(s):
        offset = (s, 0, 0)
        return remote(tile.at[0, middle], tile.at[s, middle], tile_send.at[s - 1], mid_recv.at[s - 1], offset), offset

    def col_copy(s, side):
        offset = (s, 0, 2 * side - 1)
        return remote(col_out.at[side], col_in.at[s, 1 - side], side_send.at[s, side], col_recv.at[s, 1 - side], offset), offset

    def corners(s, end):
        return pl.ds(4 * (s - 1) + 2 * end, 2)

    def corner_copy(s, side):
        offset = (s, 0, 2 * side - 1)
        return remote(
            corner_out.at[pl.ds(2 * side, 2)],
            corner_in.at[corners(s, 1 - side)],
            side_send.at[s, side],
            corner_recv.at[s - 1, 1 - side],
            offset,
        ), offset

    def part_copy(side):
        offset = (0, 2 * side - 1, 0)
        return remote(part_out.at[side], part_in.at[1 - side], part_send.at[side], part_recv.at[1 - side], offset), offset

    def start(copy, *args):
        made, offset = copy(*args)
        pl.when(inside(*offset))(made.start)

    for s in (1, 2):
        for side in (0, 1):
            start(corner_copy, s, side)
        start(edge_copy, s)
    for side in (0, 1):
        start(col_copy, 0, side)

    along = lax.broadcasted_iota(jnp.int32, (broad, chans), 0)

    def dot(a, b):
        return jnp.dot(a, b, preferred_element_type=F32)

    def spread(ref, to, s, y, beside):
        slot = {0: 0, tall - 1: 1}.get(y, y + 1)
        block = tile[s, slot * broad : (slot + 1) * broad, :].astype(F32)
        left, right = (jnp.where(inside(0, 0, 2 * end - 1), beside[end], 0.0) for end in (0, 1))
        before = jnp.where(along == 0, left, pltpu.roll(block, 1, axis=0))
        after = jnp.where(along == broad - 1, right, pltpu.roll(block, broad - 1, axis=0))
        taps = [value.astype(BF16) for value in (before, block, after)]
        if ref is None:
            return jnp.concatenate(taps, axis=1)
        for e in range(3):
            ref[to : to + broad, e * chans : (e + 1) * chans] = taps[e]

    def wait_columns(s):
        for end in (0, 1):
            pl.when(inside(0, 0, 2 * end - 1))(
                functools.partial(arrived, col_in.at[s, end], col_recv.at[s, end])
            )

    def add_part(s):
        sums = []
        for side, y in ((0, 0), (1, tall - 1)):
            if s == 0:
                beside = [col_in[0, end, y : y + 1, :].astype(F32) for end in (0, 1)]
            else:
                beside = [corner_in[4 * (s - 1) + 2 * end + side] for end in (0, 1)]
            sums.append(dot(spread(None, None, s, y, beside), weight[8 - 3 * s - 2 * side]))
        above, below = sums
        if s == 0:
            part[0] = above
            part[1] = below
        else:
            part[0] += above
            part[1] += below

    def add_tile(s):
        for y in range(tall):
            spread(window, y * broad, s, y, [col_in[s, end, y : y + 1, :].astype(F32) for end in (0, 1)])
        at = 6 - 3 * s
        total = dot(window[...], weight[at + 1])
        if s == 0:
            acc[...] = total + bias[...].reshape(1, chans)
        else:
            acc[...] += total
        acc[broad:, :] += dot(window[:last, :], weight[at])
        acc[:last, :] += dot(window[broad:, :], weight[at + 2])

    wait_columns(0)
    arrived(weight, weight_sem.at[0])
    add_part(0)
    for s in (1, 2):
        for side in (0, 1):
            start(col_copy, s, side)
        start(mid_copy, s)

    for s in (1, 2):

        @pl.when(t >= s)
        def _(s=s):
            arrived(tile.at[s, edges], edge_recv.at[s - 1])
            for end in (0, 1):
                pl.when(inside(0, 0, 2 * end - 1))(
                    functools.partial(arrived, corner_in.at[corners(s, end)], corner_recv.at[s - 1, end])
                )
            add_part(s)

    part_out[...] = part[...].astype(BF16)
    told = jnp.where(odd, beyond.astype(jnp.int32) + jnp.logical_not(above).astype(jnp.int32), 1)
    pl.when(told > 0)(functools.partial(pl.semaphore_wait, far_sem, told))
    for side in (0, 1):
        start(part_copy, side)

    add_tile(0)
    for s in (1, 2):

        @pl.when(t >= s)
        def _(s=s):
            wait_columns(s)
            arrived(tile.at[s, middle], mid_recv.at[s - 1])
            add_tile(s)

    inner = slice(broad, last)
    out_ref[inner, :] = acc[inner, :].astype(BF16)

    def sent(ref, sem, offset):
        pl.when(inside(*offset))(functools.partial(arrived, ref, sem))

    for s in (1, 2):
        sent(tile.at[0], tile_send.at[s - 1], (s, 0, 0))
    for side in (0, 1):
        sent(col_out.at[side], side_send.at[0, side], (0, 0, 2 * side - 1))
        for s in (1, 2):
            sent(corner_in.at[pl.ds(0, 2 + tall // 2)], side_send.at[s, side], (s, 0, 2 * side - 1))
        sent(part_out.at[side], part_send.at[side], (0, 2 * side - 1, 0))

    for side in (0, 1):
        there = inside(0, 2 * side - 1, 0)
        rows = slice(side * last, side * last + broad)
        pl.when(there)(functools.partial(arrived, part_in.at[side], part_recv.at[side]))
        halo = jnp.where(there, part_in[side].astype(F32), 0.0)
        out_ref[rows, :] = (acc[rows, :] + halo).astype(BF16)


def solution(mesh):
    frame_count = mesh.shape["tm"]
    tile_count = mesh.shape["tile"]

    def body(frames, norm_gain, conv_weight, conv_bias):
        _, _, tall, broad, chans = frames.shape
        pixels = tall * broad
        out = pl.pallas_call(
            functools.partial(block_kernel, tall, broad, chans, frame_count, tile_count),
            name="causal_conv",
            out_shape=pltpu.VMEM((pixels, chans), BF16),
            in_specs=[pl.BlockSpec(memory_space=pl.ANY)] * 4,
            out_specs=pl.BlockSpec(memory_space=pltpu.VMEM),
            scratch_shapes=[
                pltpu.VMEM((pixels, chans), BF16),
                pltpu.VMEM((chans,), F32),
                pltpu.VMEM((chans,), F32),
                pltpu.VMEM((9, 3 * chans, chans), BF16),
                pltpu.VMEM((3, pixels, chans), BF16),
                pltpu.VMEM((chans // LANES, pixels, LANES), F32),
                pltpu.VMEM((2, tall, chans), BF16),
                pltpu.VMEM((3, 2, tall, chans), BF16),
                pltpu.VMEM((4, 1, chans), F32),
                pltpu.VMEM((8, 1, chans), F32),
                pltpu.VMEM((2, broad, chans), BF16),
                pltpu.VMEM((2, broad, chans), BF16),
                pltpu.VMEM((pixels, 3 * chans), BF16),
                pltpu.VMEM((pixels, chans), F32),
                pltpu.VMEM((2, broad, chans), F32),
                pltpu.SemaphoreType.DMA((2,)),
                pltpu.SemaphoreType.DMA((1,)),
                pltpu.SemaphoreType.REGULAR,
                pltpu.SemaphoreType.DMA((2,)),
                pltpu.SemaphoreType.DMA((2,)),
                pltpu.SemaphoreType.DMA((2,)),
                pltpu.SemaphoreType.DMA((3, 2)),
                pltpu.SemaphoreType.DMA((2, 2)),
                pltpu.SemaphoreType.DMA((3, 2)),
                pltpu.SemaphoreType.DMA((2,)),
                pltpu.SemaphoreType.DMA((2,)),
            ],
            compiler_params=pltpu.CompilerParams(collective_id=0, has_side_effects=True),
        )(
            frames.reshape(pixels, chans),
            norm_gain,
            conv_weight.reshape(9, 3 * chans, chans),
            conv_bias,
        )
        return out.reshape(1, 1, tall, broad, chans)

    return jax.shard_map(
        body,
        mesh=mesh,
        in_specs=(P("tm", "tile", None, None, None), P(), P(), P()),
        out_specs=P("tm", "tile", None, None, None),
        check_vma=False,
    )
```

```python
import functools

import jax
import jax.numpy as jnp
from jax import lax
from jax.experimental import pallas as pl
from jax.experimental.pallas import tpu as pltpu
from jax.sharding import PartitionSpec as P

GRID_W = 8
LANES = 128
MESH = pl.DeviceIdType.MESH
F32 = jnp.float32
BF16 = jnp.bfloat16


def block_kernel(
    tall,
    broad,
    chans,
    frame_count,
    tile_count,
    frames_hbm,
    gain_hbm,
    weight_hbm,
    bias_hbm,
    out_ref,
    raw,
    gain,
    bias,
    weight,
    tile,
    act32,
    col_out,
    col_in,
    corner_out,
    corner_in,
    part_out,
    part_in,
    window,
    acc,
    part,
    measure,
    load_sem,
    weight_sem,
    far_sem,
    tile_send,
    side_send,
    part_send,
    edge_recv,
    rest_recv,
    col_recv,
    part_recv,
):
    t = lax.axis_index("tm")
    i = lax.axis_index("tile")
    row = lax.div(i, GRID_W)
    col = lax.rem(i, GRID_W)
    grid_h = tile_count // GRID_W
    pixels = tall * broad
    last = pixels - broad
    half = lax.rem(row, 2)

    loads = [
        pltpu.make_async_copy(frames_hbm, raw, load_sem.at[0]),
        pltpu.make_async_copy(gain_hbm, gain, load_sem.at[1]),
        pltpu.make_async_copy(bias_hbm, bias, load_sem.at[1]),
    ]
    for load in loads:
        load.start()

    def inside(dt, dr, dc):
        tests = []
        if dt > 0:
            tests.append(t + dt < frame_count)
        if dt < 0:
            tests.append(t + dt >= 0)
        if dr > 0:
            tests.append(row + dr < grid_h)
        if dr < 0:
            tests.append(row + dr >= 0)
        if dc > 0:
            tests.append(col + dc < GRID_W)
        if dc < 0:
            tests.append(col + dc >= 0)
        return functools.reduce(jnp.logical_and, tests)

    def signal(sem, dt, index):
        pl.semaphore_signal(sem, 1, device_id={"tm": t + dt, "tile": index}, device_id_type=MESH)

    barrier = pltpu.get_barrier_semaphore()
    partners = [(dt, dc) for dt in (-2, 2) for dc in (-1, 1)]
    partners += [(dt, 0) for dt in (-2, 2)]
    partners += [(dt, dc) for dt in (-1, 1, 0) for dc in (-1, 1)]
    partners += [(dt, 0) for dt in (-1, 1)]
    odd = half == 1
    beyond = jnp.logical_and(odd, row < grid_h - 1)
    above = i >= 2 * GRID_W
    step = GRID_W // 2
    place = lax.rem(i, 2 * GRID_W)
    half_way = jnp.logical_and(place >= step, place < 3 * step)
    signal(barrier, 0, jnp.where(odd, i - step, i + step))
    signal(barrier, 0, jnp.where(odd, jnp.where(beyond, i + 3 * step, i), jnp.where(above, i + 2 * step, i)))
    signal(barrier, 0, jnp.where(beyond, i + 4 * step, i))
    for dt, dc in partners:
        ok = inside(dt, 0, dc)
        signal(barrier, jnp.where(ok, dt, 0), jnp.where(ok, i + dc, i))
    count = len(partners) + jnp.where(odd, 0, jnp.where(above, 1, 2)) + jnp.where(jnp.logical_and(odd, jnp.logical_not(beyond)), 2, 0)
    count += jnp.where(half_way, 2 + above.astype(jnp.int32), 0)
    count += jnp.where(jnp.logical_and(odd, above), 2, 0)

    weight_loads = [
        pltpu.make_async_copy(
            weight_hbm.at[pl.ds(6 - 3 * s, 3)], weight.at[pl.ds(6 - 3 * s, 3)], weight_sem.at[0]
        )
        for s in range(3)
    ]
    for load in weight_loads:
        load.start()

    def arrived(ref, sem):
        pltpu.make_async_copy(ref, ref, sem).wait()

    def took(pixels_f32, sem):
        arrived(measure.at[pl.ds(0, pixels_f32)], sem)

    both_sides = jnp.logical_and(col > 0, col < GRID_W - 1)
    both_rows = jnp.logical_and(row > 0, row < grid_h - 1)

    def took_sides(base, each, sem):
        pl.when(both_sides)(functools.partial(took, base + 2 * each, sem))
        pl.when(jnp.logical_not(both_sides))(functools.partial(took, base + each, sem))

    loads[0].wait()
    took(2, load_sem.at[1])

    values = raw[...].astype(F32)
    scale = lax.rsqrt(jnp.mean(values * values, axis=-1, keepdims=True) + 1e-06)
    result = jax.nn.silu(values * scale * gain[...].reshape(1, chans)).astype(BF16)
    tile[0, :broad, :] = result[:broad]
    tile[0, broad : 2 * broad, :] = result[last:]
    tile[0, 2 * broad :, :] = result[broad:last]
    for j in range(chans // LANES):
        lanes = slice(j * LANES, (j + 1) * LANES)
        act32[j] = result[:, lanes].astype(F32)
        for side in (0, 1):
            column = act32[j, pl.ds(side * (broad - 1), tall, stride=broad), :]
            col_out[side, :, lanes] = column.astype(BF16)
            corner_out[2 * side, :, lanes] = column[0:1, :]
            corner_out[2 * side + 1, :, lanes] = column[tall - 1 : tall, :]

    pl.semaphore_wait(barrier, count)

    pl.when(half_way)(functools.partial(signal, far_sem, 0, i - step))
    pl.when(jnp.logical_and(half_way, jnp.logical_not(above)))(functools.partial(signal, far_sem, 0, i + step))
    pl.when(jnp.logical_and(odd, above))(functools.partial(signal, far_sem, 0, i - 4 * step))

    def remote(src, dst, send, recv, offset):
        dt, dr, dc = offset
        return pltpu.make_async_remote_copy(
            src_ref=src,
            dst_ref=dst,
            send_sem=send,
            recv_sem=recv,
            device_id={"tm": t + dt, "tile": i + dr * GRID_W + dc},
            device_id_type=MESH,
        )

    edges = pl.ds(0, 2 * broad)
    middle = pl.ds(2 * broad, pixels - 2 * broad)

    def edge_copy(s):
        offset = (s, 0, 0)
        return remote(tile.at[0, edges], tile.at[s, edges], tile_send.at[0], edge_recv.at[s - 1], offset), offset

    def mid_copy(s):
        offset = (s, 0, 0)
        return remote(tile.at[0, middle], tile.at[s, middle], tile_send.at[0], rest_recv.at[s - 1], offset), offset

    def col_copy(s, side):
        offset = (s, 0, 2 * side - 1)
        recv = rest_recv.at[s - 1] if s else col_recv.at[0]
        return remote(col_out.at[side], col_in.at[s, 1 - side], side_send.at[side], recv, offset), offset

    def corners(s, end):
        return pl.ds(4 * (s - 1) + 2 * end, 2)

    def corner_copy(s, side):
        offset = (s, 0, 2 * side - 1)
        return remote(
            corner_out.at[pl.ds(2 * side, 2)],
            corner_in.at[corners(s, 1 - side)],
            side_send.at[side],
            edge_recv.at[s - 1],
            offset,
        ), offset

    def part_copy(side):
        offset = (0, 2 * side - 1, 0)
        return remote(part_out.at[side], part_in.at[1 - side], part_send.at[0], part_recv.at[0], offset), offset

    def start(copy, *args):
        made, offset = copy(*args)
        pl.when(inside(*offset))(made.start)

    for s in (1, 2):
        for side in (0, 1):
            start(corner_copy, s, side)
        start(edge_copy, s)
    for side in (0, 1):
        start(col_copy, 0, side)

    along = lax.broadcasted_iota(jnp.int32, (broad, chans), 0)

    def dot(a, b):
        return jnp.dot(a, b, preferred_element_type=F32)

    def spread(ref, to, s, y, beside):
        slot = {0: 0, tall - 1: 1}.get(y, y + 1)
        block = tile[s, slot * broad : (slot + 1) * broad, :].astype(F32)
        left, right = (jnp.where(inside(0, 0, 2 * end - 1), beside[end], 0.0) for end in (0, 1))
        before = jnp.where(along == 0, left, pltpu.roll(block, 1, axis=0))
        after = jnp.where(along == broad - 1, right, pltpu.roll(block, broad - 1, axis=0))
        taps = [value.astype(BF16) for value in (before, block, after)]
        if ref is None:
            return jnp.concatenate(taps, axis=1)
        for e in range(3):
            ref[to : to + broad, e * chans : (e + 1) * chans] = taps[e]

    def add_part(s):
        sums = []
        for side, y in ((0, 0), (1, tall - 1)):
            if s == 0:
                beside = [col_in[0, end, y : y + 1, :].astype(F32) for end in (0, 1)]
            else:
                beside = [corner_in[4 * (s - 1) + 2 * end + side] for end in (0, 1)]
            sums.append(dot(spread(None, None, s, y, beside), weight[8 - 3 * s - 2 * side]))
        above, below = sums
        if s == 0:
            part[0] = above
            part[1] = below
        else:
            part[0] += above
            part[1] += below

    def add_tile(s):
        for y in range(tall):
            spread(window, y * broad, s, y, [col_in[s, end, y : y + 1, :].astype(F32) for end in (0, 1)])
        at = 6 - 3 * s
        total = dot(window[...], weight[at + 1])
        if s == 0:
            acc[...] = total + bias[...].reshape(1, chans)
        else:
            acc[...] += total
        acc[broad:, :] += dot(window[:last, :], weight[at])
        acc[:last, :] += dot(window[broad:, :], weight[at + 2])

    took_sides(0, tall // 2, col_recv.at[0])
    arrived(weight, weight_sem.at[0])
    add_part(0)
    for s in (1, 2):
        for side in (0, 1):
            start(col_copy, s, side)
        start(mid_copy, s)

    for s in (1, 2):

        @pl.when(t >= s)
        def _(s=s):
            took_sides(broad, 2, edge_recv.at[s - 1])
            add_part(s)

    part_out[...] = part[...].astype(BF16)
    greeted = jnp.logical_and(odd, above)
    up = part_copy(0)[0]
    pl.when(greeted)(up.start)
    told = jnp.where(odd, beyond.astype(jnp.int32) + jnp.logical_not(above).astype(jnp.int32), 1)
    pl.when(told > 0)(functools.partial(pl.semaphore_wait, far_sem, told))
    pl.when(jnp.logical_and(inside(0, -1, 0), jnp.logical_not(greeted)))(up.start)
    start(part_copy, 1)

    add_tile(0)
    for s in (1, 2):

        @pl.when(t >= s)
        def _(s=s):
            took_sides((pixels - 2 * broad) // 2, tall // 2, rest_recv.at[s - 1])
            add_tile(s)

    inner = slice(broad, last)
    out_ref[inner, :] = acc[inner, :].astype(BF16)

    pl.when(t < frame_count - 2)(functools.partial(arrived, tile.at[pl.ds(0, 2)], tile_send.at[0]))
    pl.when(t == frame_count - 2)(functools.partial(arrived, tile.at[0], tile_send.at[0]))
    for side in (0, 1):
        there = inside(0, 0, 2 * side - 1)
        for later in range(3):
            holds = t == frame_count - 1 - later if later < 2 else t < frame_count - 2
            pl.when(jnp.logical_and(there, holds))(
                functools.partial(took, tall // 2 + later * (tall // 2 + 2), side_send.at[side])
            )
    pl.when(both_rows)(functools.partial(arrived, part_out, part_send.at[0]))
    pl.when(jnp.logical_not(both_rows))(functools.partial(arrived, part_out.at[0], part_send.at[0]))

    pl.when(both_rows)(functools.partial(arrived, part_in, part_recv.at[0]))
    pl.when(jnp.logical_not(both_rows))(functools.partial(arrived, part_in.at[0], part_recv.at[0]))
    for side in (0, 1):
        there = inside(0, 2 * side - 1, 0)
        rows = slice(side * last, side * last + broad)
        halo = jnp.where(there, part_in[side].astype(F32), 0.0)
        out_ref[rows, :] = (acc[rows, :] + halo).astype(BF16)


def solution(mesh):
    frame_count = mesh.shape["tm"]
    tile_count = mesh.shape["tile"]

    def body(frames, norm_gain, conv_weight, conv_bias):
        _, _, tall, broad, chans = frames.shape
        pixels = tall * broad
        out = pl.pallas_call(
            functools.partial(block_kernel, tall, broad, chans, frame_count, tile_count),
            name="causal_conv",
            out_shape=pltpu.VMEM((pixels, chans), BF16),
            in_specs=[pl.BlockSpec(memory_space=pl.ANY)] * 4,
            out_specs=pl.BlockSpec(memory_space=pltpu.VMEM),
            scratch_shapes=[
                pltpu.VMEM((pixels, chans), BF16),
                pltpu.VMEM((chans,), F32),
                pltpu.VMEM((chans,), F32),
                pltpu.VMEM((9, 3 * chans, chans), BF16),
                pltpu.VMEM((3, pixels, chans), BF16),
                pltpu.VMEM((chans // LANES, pixels, LANES), F32),
                pltpu.VMEM((2, tall, chans), BF16),
                pltpu.VMEM((3, 2, tall, chans), BF16),
                pltpu.VMEM((4, 1, chans), F32),
                pltpu.VMEM((8, 1, chans), F32),
                pltpu.VMEM((2, broad, chans), BF16),
                pltpu.VMEM((2, broad, chans), BF16),
                pltpu.VMEM((pixels, 3 * chans), BF16),
                pltpu.VMEM((pixels, chans), F32),
                pltpu.VMEM((2, broad, chans), F32),
                pltpu.VMEM(((pixels - 2 * broad) // 2 + tall, 1, chans), F32),
                pltpu.SemaphoreType.DMA((2,)),
                pltpu.SemaphoreType.DMA((1,)),
                pltpu.SemaphoreType.REGULAR,
                pltpu.SemaphoreType.DMA((1,)),
                pltpu.SemaphoreType.DMA((2,)),
                pltpu.SemaphoreType.DMA((1,)),
                pltpu.SemaphoreType.DMA((2,)),
                pltpu.SemaphoreType.DMA((2,)),
                pltpu.SemaphoreType.DMA((1,)),
                pltpu.SemaphoreType.DMA((1,)),
            ],
            compiler_params=pltpu.CompilerParams(collective_id=0, has_side_effects=True),
        )(
            frames.reshape(pixels, chans),
            norm_gain,
            conv_weight.reshape(9, 3 * chans, chans),
            conv_bias,
        )
        return out.reshape(1, 1, tall, broad, chans)

    return jax.shard_map(
        body,
        mesh=mesh,
        in_specs=(P("tm", "tile", None, None, None), P(), P(), P()),
        out_specs=P("tm", "tile", None, None, None),
        check_vma=False,
    )
```

```python
import functools

import jax
import jax.numpy as jnp
from jax import lax
from jax.experimental import pallas as pl
from jax.experimental.pallas import tpu as pltpu
from jax.sharding import PartitionSpec as P

GRID_W = 8
LANES = 128
MESH = pl.DeviceIdType.MESH
F32 = jnp.float32
BF16 = jnp.bfloat16


def block_kernel(
    tall,
    broad,
    chans,
    frame_count,
    tile_count,
    frames_hbm,
    gain_hbm,
    weight_hbm,
    bias_hbm,
    out_ref,
    raw,
    gain,
    bias,
    weight,
    tile,
    act32,
    col_out,
    col_in,
    corner_out,
    corner_in,
    part_out,
    part_in,
    window,
    acc,
    part,
    measure,
    load_sem,
    weight_sem,
    far_sem,
    tile_send,
    side_send,
    part_send,
    edge_recv,
    rest_recv,
    col_recv,
    part_recv,
):
    t = lax.axis_index("tm")
    i = lax.axis_index("tile")
    row = lax.div(i, GRID_W)
    col = lax.rem(i, GRID_W)
    grid_h = tile_count // GRID_W
    pixels = tall * broad
    last = pixels - broad
    half = lax.rem(row, 2)

    loads = [
        pltpu.make_async_copy(frames_hbm, raw, load_sem.at[0]),
        pltpu.make_async_copy(gain_hbm, gain, load_sem.at[1]),
        pltpu.make_async_copy(bias_hbm, bias, load_sem.at[1]),
    ]
    for load in loads:
        load.start()

    def inside(dt, dr, dc):
        tests = []
        if dt > 0:
            tests.append(t + dt < frame_count)
        if dt < 0:
            tests.append(t + dt >= 0)
        if dr > 0:
            tests.append(row + dr < grid_h)
        if dr < 0:
            tests.append(row + dr >= 0)
        if dc > 0:
            tests.append(col + dc < GRID_W)
        if dc < 0:
            tests.append(col + dc >= 0)
        return functools.reduce(jnp.logical_and, tests)

    def signal(sem, dt, index):
        pl.semaphore_signal(sem, 1, device_id={"tm": t + dt, "tile": index}, device_id_type=MESH)

    barrier = pltpu.get_barrier_semaphore()
    partners = [(dt, dc) for dt in (-2, 2) for dc in (-1, 1)]
    partners += [(dt, 0) for dt in (-2, 2)]
    partners += [(dt, dc) for dt in (-1, 1, 0) for dc in (-1, 1)]
    partners += [(dt, 0) for dt in (-1, 1)]
    odd = half == 1
    beyond = jnp.logical_and(odd, row < grid_h - 1)
    above = i >= 2 * GRID_W
    step = GRID_W // 2
    place = lax.rem(i, 2 * GRID_W)
    half_way = jnp.logical_and(place >= step, place < 3 * step)
    signal(barrier, 0, jnp.where(odd, i - step, i + step))
    signal(barrier, 0, jnp.where(odd, jnp.where(beyond, i + 3 * step, i), jnp.where(above, i + 2 * step, i)))
    signal(barrier, 0, jnp.where(beyond, i + 4 * step, i))
    for dt, dc in partners:
        ok = inside(dt, 0, dc)
        signal(barrier, jnp.where(ok, dt, 0), jnp.where(ok, i + dc, i))
    count = len(partners) + jnp.where(odd, 0, jnp.where(above, 1, 2)) + jnp.where(jnp.logical_and(odd, jnp.logical_not(beyond)), 2, 0)
    count += jnp.where(half_way, 2 + above.astype(jnp.int32), 0)
    count += jnp.where(jnp.logical_and(odd, above), 2, 0)

    weight_loads = [
        pltpu.make_async_copy(
            weight_hbm.at[pl.ds(6 - 3 * s, 3)], weight.at[pl.ds(6 - 3 * s, 3)], weight_sem.at[0]
        )
        for s in range(3)
    ]
    for load in weight_loads:
        load.start()

    def arrived(ref, sem):
        pltpu.make_async_copy(ref, ref, sem).wait()

    def took(pixels_f32, sem):
        arrived(measure.at[pl.ds(0, pixels_f32)], sem)

    both_sides = jnp.logical_and(col > 0, col < GRID_W - 1)
    both_rows = jnp.logical_and(row > 0, row < grid_h - 1)

    def took_sides(base, each, sem):
        pl.when(both_sides)(functools.partial(took, base + 2 * each, sem))
        pl.when(jnp.logical_not(both_sides))(functools.partial(took, base + each, sem))

    loads[0].wait()
    took(2, load_sem.at[1])

    values = raw[...].astype(F32)
    scale = lax.rsqrt(jnp.mean(values * values, axis=-1, keepdims=True) + 1e-06)
    result = jax.nn.silu(values * scale * gain[...].reshape(1, chans)).astype(BF16)
    tile[0, :broad, :] = result[:broad]
    tile[0, broad : 2 * broad, :] = result[last:]
    tile[0, 2 * broad :, :] = result[broad:last]
    for j in range(chans // LANES):
        lanes = slice(j * LANES, (j + 1) * LANES)
        act32[j] = result[:, lanes].astype(F32)
        for side in (0, 1):
            column = act32[j, pl.ds(side * (broad - 1), tall, stride=broad), :]
            col_out[side, :, lanes] = column.astype(BF16)
            corner_out[2 * side, :, lanes] = column[0:1, :]
            corner_out[2 * side + 1, :, lanes] = column[tall - 1 : tall, :]

    pl.semaphore_wait(barrier, count)

    pl.when(half_way)(functools.partial(signal, far_sem, 0, i - step))
    pl.when(jnp.logical_and(half_way, jnp.logical_not(above)))(functools.partial(signal, far_sem, 0, i + step))
    pl.when(jnp.logical_and(odd, above))(functools.partial(signal, far_sem, 0, i - 4 * step))

    def remote(src, dst, send, recv, offset):
        dt, dr, dc = offset
        return pltpu.make_async_remote_copy(
            src_ref=src,
            dst_ref=dst,
            send_sem=send,
            recv_sem=recv,
            device_id={"tm": t + dt, "tile": i + dr * GRID_W + dc},
            device_id_type=MESH,
        )

    edges = pl.ds(0, 2 * broad)
    middle = pl.ds(2 * broad, pixels - 2 * broad)

    def edge_copy(s):
        offset = (s, 0, 0)
        return remote(tile.at[0, edges], tile.at[s, edges], tile_send.at[0], edge_recv.at[s - 1], offset), offset

    def mid_copy(s):
        offset = (s, 0, 0)
        return remote(tile.at[0, middle], tile.at[s, middle], tile_send.at[0], rest_recv.at[s - 1], offset), offset

    def col_copy(s, side):
        offset = (s, 0, 2 * side - 1)
        recv = rest_recv.at[s - 1] if s else col_recv.at[0]
        return remote(col_out.at[side], col_in.at[s, 1 - side], side_send.at[side], recv, offset), offset

    def corners(s, end):
        return pl.ds(4 * (s - 1) + 2 * end, 2)

    def corner_copy(s, side):
        offset = (s, 0, 2 * side - 1)
        return remote(
            corner_out.at[pl.ds(2 * side, 2)],
            corner_in.at[corners(s, 1 - side)],
            side_send.at[side],
            edge_recv.at[s - 1],
            offset,
        ), offset

    def part_copy(side):
        offset = (0, 2 * side - 1, 0)
        return remote(part_out.at[side], part_in.at[1 - side], part_send.at[0], part_recv.at[0], offset), offset

    def start(copy, *args):
        made, offset = copy(*args)
        pl.when(inside(*offset))(made.start)

    for s in (1, 2):
        for side in (0, 1):
            start(corner_copy, s, side)
        start(edge_copy, s)
    for side in (0, 1):
        start(col_copy, 0, side)

    along = lax.broadcasted_iota(jnp.int32, (broad, chans), 0)

    def dot(a, b):
        return jnp.dot(a, b, preferred_element_type=F32)

    def spread(ref, to, s, y, beside):
        slot = {0: 0, tall - 1: 1}.get(y, y + 1)
        block = tile[s, slot * broad : (slot + 1) * broad, :].astype(F32)
        left, right = (jnp.where(inside(0, 0, 2 * end - 1), beside[end], 0.0) for end in (0, 1))
        before = jnp.where(along == 0, left, pltpu.roll(block, 1, axis=0))
        after = jnp.where(along == broad - 1, right, pltpu.roll(block, broad - 1, axis=0))
        taps = [value.astype(BF16) for value in (before, block, after)]
        if ref is None:
            return jnp.concatenate(taps, axis=1)
        for e in range(3):
            ref[to : to + broad, e * chans : (e + 1) * chans] = taps[e]

    told = jnp.where(odd, beyond.astype(jnp.int32) + jnp.logical_not(above).astype(jnp.int32), 1)

    def add_side(s, side):
        y = side * (tall - 1)
        if s == 0:
            beside = [col_in[0, end, y : y + 1, :].astype(F32) for end in (0, 1)]
        else:
            beside = [corner_in[4 * (s - 1) + 2 * end + side] for end in (0, 1)]
        term = dot(spread(None, None, s, y, beside), weight[8 - 3 * s - 2 * side])
        part[side] = term if s == 0 else part[side] + term

    def add_part(s):
        add_side(s, 0)
        add_side(s, 1)

    def finish(s):
        add_side(s, 1)
        part_out[1] = part[1].astype(BF16)
        pl.when(told > 0)(functools.partial(pl.semaphore_wait, far_sem, told))
        start(part_copy, 1)
        add_side(s, 0)
        part_out[0] = part[0].astype(BF16)
        start(part_copy, 0)

    def add_tile(s):
        for y in range(tall):
            spread(window, y * broad, s, y, [col_in[s, end, y : y + 1, :].astype(F32) for end in (0, 1)])
        at = 6 - 3 * s
        total = dot(window[...], weight[at + 1])
        if s == 0:
            acc[...] = total + bias[...].reshape(1, chans)
        else:
            acc[...] += total
        acc[broad:, :] += dot(window[:last, :], weight[at])
        acc[:last, :] += dot(window[broad:, :], weight[at + 2])

    took_sides(0, tall // 2, col_recv.at[0])
    arrived(weight, weight_sem.at[0])
    add_part(0)
    for s in (1, 2):
        for side in (0, 1):
            start(col_copy, s, side)
        start(mid_copy, s)

    for s in (1, 2):

        @pl.when(t >= s)
        def _(s=s):
            took_sides(broad, 2, edge_recv.at[s - 1])
            if s == 1:
                pl.when(t == 1)(functools.partial(finish, 1))
                pl.when(t > 1)(functools.partial(add_part, 1))
            else:
                finish(s)

    @pl.when(t == 0)
    def _():
        part_out[...] = part[...].astype(BF16)
        greeted = jnp.logical_and(odd, above)
        up = part_copy(0)[0]
        pl.when(greeted)(up.start)
        pl.when(told > 0)(functools.partial(pl.semaphore_wait, far_sem, told))
        pl.when(jnp.logical_and(inside(0, -1, 0), jnp.logical_not(greeted)))(up.start)
        start(part_copy, 1)

    add_tile(0)
    for s in (1, 2):

        @pl.when(t >= s)
        def _(s=s):
            took_sides((pixels - 2 * broad) // 2, tall // 2, rest_recv.at[s - 1])
            add_tile(s)

    inner = slice(broad, last)
    out_ref[inner, :] = acc[inner, :].astype(BF16)

    pl.when(t < frame_count - 2)(functools.partial(arrived, tile.at[pl.ds(0, 2)], tile_send.at[0]))
    pl.when(t == frame_count - 2)(functools.partial(arrived, tile.at[0], tile_send.at[0]))
    for side in (0, 1):
        there = inside(0, 0, 2 * side - 1)
        for later in range(3):
            holds = t == frame_count - 1 - later if later < 2 else t < frame_count - 2
            pl.when(jnp.logical_and(there, holds))(
                functools.partial(took, tall // 2 + later * (tall // 2 + 2), side_send.at[side])
            )
    pl.when(both_rows)(functools.partial(arrived, part_out, part_send.at[0]))
    pl.when(jnp.logical_not(both_rows))(functools.partial(arrived, part_out.at[0], part_send.at[0]))

    pl.when(both_rows)(functools.partial(arrived, part_in, part_recv.at[0]))
    pl.when(jnp.logical_not(both_rows))(functools.partial(arrived, part_in.at[0], part_recv.at[0]))
    for side in (0, 1):
        there = inside(0, 2 * side - 1, 0)
        rows = slice(side * last, side * last + broad)
        halo = jnp.where(there, part_in[side].astype(F32), 0.0)
        out_ref[rows, :] = (acc[rows, :] + halo).astype(BF16)


def solution(mesh):
    frame_count = mesh.shape["tm"]
    tile_count = mesh.shape["tile"]

    def body(frames, norm_gain, conv_weight, conv_bias):
        _, _, tall, broad, chans = frames.shape
        pixels = tall * broad
        out = pl.pallas_call(
            functools.partial(block_kernel, tall, broad, chans, frame_count, tile_count),
            name="causal_conv",
            out_shape=pltpu.VMEM((pixels, chans), BF16),
            in_specs=[pl.BlockSpec(memory_space=pl.ANY)] * 4,
            out_specs=pl.BlockSpec(memory_space=pltpu.VMEM),
            scratch_shapes=[
                pltpu.VMEM((pixels, chans), BF16),
                pltpu.VMEM((chans,), F32),
                pltpu.VMEM((chans,), F32),
                pltpu.VMEM((9, 3 * chans, chans), BF16),
                pltpu.VMEM((3, pixels, chans), BF16),
                pltpu.VMEM((chans // LANES, pixels, LANES), F32),
                pltpu.VMEM((2, tall, chans), BF16),
                pltpu.VMEM((3, 2, tall, chans), BF16),
                pltpu.VMEM((4, 1, chans), F32),
                pltpu.VMEM((8, 1, chans), F32),
                pltpu.VMEM((2, broad, chans), BF16),
                pltpu.VMEM((2, broad, chans), BF16),
                pltpu.VMEM((pixels, 3 * chans), BF16),
                pltpu.VMEM((pixels, chans), F32),
                pltpu.VMEM((2, broad, chans), F32),
                pltpu.VMEM(((pixels - 2 * broad) // 2 + tall, 1, chans), F32),
                pltpu.SemaphoreType.DMA((2,)),
                pltpu.SemaphoreType.DMA((1,)),
                pltpu.SemaphoreType.REGULAR,
                pltpu.SemaphoreType.DMA((1,)),
                pltpu.SemaphoreType.DMA((2,)),
                pltpu.SemaphoreType.DMA((1,)),
                pltpu.SemaphoreType.DMA((2,)),
                pltpu.SemaphoreType.DMA((2,)),
                pltpu.SemaphoreType.DMA((1,)),
                pltpu.SemaphoreType.DMA((1,)),
            ],
            compiler_params=pltpu.CompilerParams(collective_id=0, has_side_effects=True),
        )(
            frames.reshape(pixels, chans),
            norm_gain,
            conv_weight.reshape(9, 3 * chans, chans),
            conv_bias,
        )
        return out.reshape(1, 1, tall, broad, chans)

    return jax.shard_map(
        body,
        mesh=mesh,
        in_specs=(P("tm", "tile", None, None, None), P(), P(), P()),
        out_specs=P("tm", "tile", None, None, None),
        check_vma=False,
    )
```
